32 devices in a mesh: gx: 8 (over y, x, core), gy: 4 (over z).
Axes of the slice: x: 2, y: 2, z: 4, core: 2. Of those that a mesh axis runs over, the one named last changes fastest.
Arguments:
- right_side: float32 [3, 128, 32, 256], P(None, 'gx', 'gy'), may hold values from -12 to 12
- labels: int32 [128, 32, 256], P('gx', 'gy'), may hold values 0 or 1
Outputs:
- solution: float32 [3, 128, 32, 256], P(None, 'gx', 'gy')
- residual: float32 [3, 128, 32, 256], P(None, 'gx', 'gy')
The draws below stay inside these ranges and needn't reach their ends.
All inputs are finite; a program needn't handle non-finite values. No bound on the sum of `labels` on one device may be relied on, other than what follows from the above.
Results may differ from the reference program's by a relative error of at most 0.0003.
Values sent between devices are 32-bit elements; how exact they have to be, the bound alone decides.
A program may use at most 64 MiB of HBM per device.

```python
import math
import jax
import jax.numpy as jnp
import numpy as np
from jax import lax

NZ = 256
ITERS = 4
NX = 128
NY = 32


def draw_right_side(key, part):
    key_base = jax.random.fold_in(jax.random.fold_in(key, 11), 0)
    position_x = jnp.arange(NX, dtype=jnp.float32) / NX
    position_y = jnp.arange(NY, dtype=jnp.float32) / NY
    base_values = jnp.clip(jax.random.normal(key_base, (3, NX, NY, NZ), jnp.float32), -4.0, 4.0)
    amplitude = jnp.exp(math.log(3.0) * (0.5 * position_x[:, None] + 0.5 * position_y[None, :]))
    values = base_values * amplitude[None, :, :, None]
    return values.astype(jnp.float32)


def place_ends(entries, own_key, smallest, largest):
    dims = entries.shape
    spot = [jax.random.randint(jax.random.fold_in(own_key, axis), (), 0, dims[axis]) for axis in range(len(dims))]
    entries = entries.at[tuple(spot)].set(smallest)
    longest = dims.index(max(dims))
    spot[longest] = (spot[longest] + 1) % dims[longest]
    return entries.at[tuple(spot)].set(largest)


def setup_inputs(seed: int = 0) -> dict:
    key_list = jax.random.split(jax.random.key(seed), 3)
    return {
        "right_side": draw_right_side(jax.random.fold_in(key_list[2], 71), 0),
        "labels": place_ends((jax.random.randint(key_list[1], (NX, NY, NZ), 0, 3) < 1).astype(jnp.int32), jax.random.fold_in(key_list[1], 1), 0, 1),
    }


LAMBDA_SOFT = 0.5769231
LAMBDA_RISE = 1.6452991
SHEAR_SOFT = 0.3846154
SHEAR_RISE = 2.9487179
KAPPA = 0.05

def corner_bits(corner):
    return (corner >> 2 & 1, corner >> 1 & 1, corner & 1)

def element_tables():
    gauss_offset = 0.5 / math.sqrt(3.0)
    gauss_points = [0.5 - gauss_offset, 0.5 + gauss_offset]
    lame_table = np.zeros((24, 24))
    shear_table = np.zeros((24, 24))
    normal_block = np.zeros((6, 6))
    normal_block[:3, :3] = 1.0
    shear_block = np.zeros((6, 6))
    for entry in range(6):
        shear_block[entry, entry] = 2.0 if entry < 3 else 1.0
    for point_x in gauss_points:
        for point_y in gauss_points:
            for point_z in gauss_points:
                strain = np.zeros((6, 24))
                for corner in range(8):
                    cx_bit, cy_bit, cz_bit = corner_bits(corner)
                    shape_x = point_x if cx_bit else 1.0 - point_x
                    shape_y = point_y if cy_bit else 1.0 - point_y
                    shape_z = point_z if cz_bit else 1.0 - point_z
                    slope_x = 1.0 if cx_bit else -1.0
                    slope_y = 1.0 if cy_bit else -1.0
                    slope_z = 1.0 if cz_bit else -1.0
                    grad_x = slope_x * shape_y * shape_z
                    grad_y = shape_x * slope_y * shape_z
                    grad_z = shape_x * shape_y * slope_z
                    column = 3 * corner
                    strain[0, column] = grad_x
                    strain[1, column + 1] = grad_y
                    strain[2, column + 2] = grad_z
                    strain[3, column + 1] = grad_z
                    strain[3, column + 2] = grad_y
                    strain[4, column] = grad_z
                    strain[4, column + 2] = grad_x
                    strain[5, column] = grad_y
                    strain[5, column + 1] = grad_x
                lame_table += 0.125 * strain.T @ normal_block @ strain
                shear_table += 0.125 * strain.T @ shear_block @ strain
    return np.concatenate([lame_table, shear_table], 0).astype(np.float32)

def table_diagonal(table):
    return np.array([table[entry, entry] for entry in range(24)], dtype=np.float32)

def moduli(labels):
    stiff = labels.astype(jnp.float32)
    return (LAMBDA_SOFT + LAMBDA_RISE * stiff, SHEAR_SOFT + SHEAR_RISE * stiff)

def reference(right_side, labels):
    tables = element_tables()
    stiffness = jnp.asarray(tables, dtype=jnp.float32)
    diag_lame = jnp.asarray(table_diagonal(tables[:24]), dtype=jnp.float32)
    diag_shear = jnp.asarray(table_diagonal(tables[24:]), dtype=jnp.float32)
    lame_first, shear_modulus = moduli(labels)
    row_block = math.gcd(NX, 8)
    block_count = NX // row_block

    def operate(vector_in):
        wrapped = jnp.concatenate([vector_in, vector_in[:, :1]], 1)

        def one_block(number):
            offset = number * row_block
            node_values = lax.dynamic_slice_in_dim(wrapped, offset, row_block + 1, 1)
            lame_block = lax.dynamic_slice_in_dim(lame_first, offset, row_block, 0)
            shear_part = lax.dynamic_slice_in_dim(shear_modulus, offset, row_block, 0)
            rolled_z = jnp.roll(node_values, -1, 3)
            corner_views = []
            for corner in range(8):
                cx_bit, cy_bit, cz_bit = corner_bits(corner)
                source_nodes = rolled_z if cz_bit else node_values
                corner_view = source_nodes[:, cx_bit:cx_bit + row_block]
                if cy_bit:
                    corner_view = jnp.roll(corner_view, -1, 2)
                corner_views.append(corner_view)
            stacked = jnp.concatenate(corner_views, 0).reshape(24, -1)
            products = jnp.dot(stiffness, stacked, precision=lax.Precision.HIGHEST, preferred_element_type=jnp.float32)
            forces = (lame_block.reshape(1, -1) * products[:24] + shear_part.reshape(1, -1) * products[24:]).reshape(8, 3, row_block, NY, NZ)
            lower_sum = jnp.zeros((3, row_block, NY, NZ), jnp.float32)
            upper_sum = jnp.zeros((3, row_block, NY, NZ), jnp.float32)
            for corner in range(8):
                cx_bit, cy_bit, cz_bit = corner_bits(corner)
                portion = forces[corner]
                if cy_bit:
                    portion = jnp.roll(portion, 1, 2)
                if cz_bit:
                    portion = jnp.roll(portion, 1, 3)
                if cx_bit:
                    upper_sum = upper_sum + portion
                else:
                    lower_sum = lower_sum + portion
            return (lower_sum, upper_sum)
        lower_sum, upper_sum = lax.map(one_block, jnp.arange(block_count, dtype=jnp.int32))
        lower_sum = jnp.moveaxis(lower_sum, 0, 1).reshape(3, NX, NY, NZ)
        upper_sum = jnp.moveaxis(upper_sum, 0, 1).reshape(3, NX, NY, NZ)
        return lower_sum + jnp.roll(upper_sum, 1, 1) + KAPPA * vector_in
    diagonal = jnp.zeros((3, NX, NY, NZ), jnp.float32) + KAPPA
    for corner in range(8):
        cx_bit, cy_bit, cz_bit = corner_bits(corner)
        portion = lame_first[None] * diag_lame[3 * corner:3 * corner + 3, None, None, None] + shear_modulus[None] * diag_shear[3 * corner:3 * corner + 3, None, None, None]
        portion = jnp.roll(portion, (cx_bit, cy_bit, cz_bit), (1, 2, 3))
        diagonal = diagonal + portion
    solution = jnp.zeros_like(right_side)
    residual = right_side
    scaled = residual / diagonal
    direction = scaled
    descent = jnp.sum(residual * scaled)
    for iteration in range(ITERS):
        image_vector = operate(direction)
        step_length = descent / jnp.sum(direction * image_vector)
        solution = solution + step_length * direction
        residual = residual - step_length * image_vector
        scaled = residual / diagonal
        descent_new = jnp.sum(residual * scaled)
        direction = scaled + descent_new / descent * direction
        descent = descent_new
    return (solution, residual)
```

```python
import functools
import math

import jax
import jax.numpy as jnp
import numpy as np
from jax import lax
from jax.experimental import pallas as pl
from jax.experimental.pallas import tpu as pltpu
from jax.sharding import PartitionSpec as P

ITERS = 4

LAMBDA_SOFT = 0.5769231
LAMBDA_RISE = 1.6452991
SHEAR_SOFT = 0.3846154
SHEAR_RISE = 2.9487179
KAPPA = 0.05
PIVOT_FLOOR = 1e-6
SHIFTS = (1.0, 1.4, 1.4)
MIXES = (0.0, 0.3, 0.45)

MESH = pl.DeviceIdType.MESH
F32 = jnp.float32


def corner_bits(corner):
    return (corner >> 2 & 1, corner >> 1 & 1, corner & 1)


def element_tables():
    gauss_offset = 0.5 / math.sqrt(3.0)
    gauss_points = [0.5 - gauss_offset, 0.5 + gauss_offset]
    lame_table = np.zeros((24, 24))
    shear_table = np.zeros((24, 24))
    normal_block = np.zeros((6, 6))
    normal_block[:3, :3] = 1.0
    shear_block = np.diag([2.0, 2.0, 2.0, 1.0, 1.0, 1.0])
    for point_x in gauss_points:
        for point_y in gauss_points:
            for point_z in gauss_points:
                strain = np.zeros((6, 24))
                for corner in range(8):
                    cx_bit, cy_bit, cz_bit = corner_bits(corner)
                    shape_x = point_x if cx_bit else 1.0 - point_x
                    shape_y = point_y if cy_bit else 1.0 - point_y
                    shape_z = point_z if cz_bit else 1.0 - point_z
                    slope_x = 1.0 if cx_bit else -1.0
                    slope_y = 1.0 if cy_bit else -1.0
                    slope_z = 1.0 if cz_bit else -1.0
                    grad_x = slope_x * shape_y * shape_z
                    grad_y = shape_x * slope_y * shape_z
                    grad_z = shape_x * shape_y * slope_z
                    column = 3 * corner
                    strain[0, column] = grad_x
                    strain[1, column + 1] = grad_y
                    strain[2, column + 2] = grad_z
                    strain[3, column + 1] = grad_z
                    strain[3, column + 2] = grad_y
                    strain[4, column] = grad_z
                    strain[4, column + 2] = grad_x
                    strain[5, column] = grad_y
                    strain[5, column + 1] = grad_x
                lame_table += 0.125 * strain.T @ normal_block @ strain
                shear_table += 0.125 * strain.T @ shear_block @ strain
    return lame_table, shear_table


def diagonal_weights():
    lame_table, shear_table = element_tables()
    lame, shear = np.diag(lame_table), np.diag(shear_table)
    assert np.allclose(lame, lame[0]) and np.allclose(shear, shear[0])
    soft = LAMBDA_SOFT * lame[0] + SHEAR_SOFT * shear[0]
    rise = LAMBDA_RISE * lame[0] + SHEAR_RISE * shear[0]
    return float(8.0 * soft + KAPPA), float(rise)


def voxel_forces(lower, upper, stiff):
    l0 = LAMBDA_SOFT / 16.0 + LAMBDA_RISE / 16.0 * stiff
    m0 = SHEAR_SOFT / 16.0 + SHEAR_RISE / 16.0 * stiff
    l1, m1 = l0 * (1.0 / 3.0), m0 * (1.0 / 3.0)
    q = (l1 + 4.0 * m1) * (1.0 / 3.0)
    m0_2 = m0 + m0
    m1_3 = m0
    fx, fy, fz, fxy, fxz, fyz, fxyz = ([None] * 3 for _ in range(7))
    ex, ey, ez, exy, exz, eyz = ([None] * 3 for _ in range(6))
    for c in range(3):
        a, b = lower[4 * c : 4 * c + 4], upper[4 * c : 4 * c + 4]
        ex[c] = b[0] - a[0]
        ey[c], exy[c] = a[1] + b[1], b[1] - a[1]
        ez[c], exz[c] = a[2] + b[2], b[2] - a[2]
        eyz[c] = a[3] + b[3]
        fxyz[c] = q * (b[3] - a[3])
    trace = l0 * (ex[0] + ey[1] + ez[2])
    fx[0] = trace + m0_2 * ex[0]
    fy[1] = trace + m0_2 * ey[1]
    fz[2] = trace + m0_2 * ez[2]
    fy[0] = fx[1] = m0 * (ey[0] + ex[1])
    fz[0] = fx[2] = m0 * (ez[0] + ex[2])
    fz[1] = fy[2] = m0 * (ez[1] + ey[2])
    part = l1 * (exy[0] + eyz[2])
    fxy[0], fyz[2] = part + m1_3 * exy[0], part + m1_3 * eyz[2]
    part = l1 * (exy[1] + exz[2])
    fxy[1], fxz[2] = part + m1_3 * exy[1], part + m1_3 * exz[2]
    part = l1 * (exz[0] + eyz[1])
    fxz[0], fyz[1] = part + m1_3 * exz[0], part + m1_3 * eyz[1]
    total = eyz[0] + exz[1] + exy[2]
    fyz[0] = m1 * (total + eyz[0])
    fxz[1] = m1 * (total + exz[1])
    fxy[2] = m1 * (total + exy[2])
    low, high = [], []
    for c in range(3):
        low += [-fx[c], fy[c] - fxy[c], fz[c] - fxz[c], fyz[c] - fxyz[c]]
        high += [fx[c], fy[c] + fxy[c], fz[c] + fxz[c], fyz[c] + fxyz[c]]
    return low, high


def cg_kernel(nx, ny, cx, cy, nz, rhs_hbm, lab_hbm, sol_ref, res_ref,
              bvec, zvec, vvec, lab, stiff, rinv, comb, forc, ysend, yrecv, csend, crecv,
              psend, precv, in_sem, send_sem, recv_sem, lsend_sem, lrecv_sem,
              rsend_sem, rrecv_sem):
    rows = cy + 8
    n = nx * ny
    gx, gy = lax.axis_index("gx"), lax.axis_index("gy")
    me = gx * ny + gy
    xs = {-1: lax.rem(gx + nx - 1, nx), 0: gx, 1: lax.rem(gx + 1, nx)}
    ys = {-1: lax.rem(gy + ny - 1, ny), 0: gy, 1: lax.rem(gy + 1, ny)}

    load_b = pltpu.make_async_copy(
        rhs_hbm, bvec.at[:, pl.ds(1, cx), pl.ds(0, cy), :], in_sem.at[0])
    load_l = pltpu.make_async_copy(
        lab_hbm, lab.at[pl.ds(2, cx), pl.ds(0, cy), :], in_sem.at[1])
    load_b.start()
    load_l.start()

    barrier = pltpu.get_barrier_semaphore()

    def greet(k, _):
        other = lax.rem(me + k, n)
        pl.semaphore_signal(barrier, inc=1, device_id=(other // ny, lax.rem(other, ny)),
                            device_id_type=MESH)
        return 0

    lax.fori_loop(1, n, greet, 0)
    load_b.wait()
    load_l.wait()

    sides = (1, -1)
    corners = ((1, 1), (1, -1), (-1, 1), (-1, -1))
    pending = []

    def remote(src, dst, s_sem, r_sem, dx, dy):
        copy = pltpu.make_async_remote_copy(
            src_ref=src, dst_ref=dst, send_sem=s_sem, recv_sem=r_sem,
            device_id=(xs[dx], ys[dy]), device_id_type=MESH)
        copy.start()
        pending.append(copy)
        return copy

    def exchange(turn, vec, depth):
        copies = []
        for k, side in enumerate(sides):
            parts = depth[k]
            copies.append(remote(ysend.at[turn, k, pl.ds(0, parts)],
                                 yrecv.at[turn, k, pl.ds(0, parts)],
                                 send_sem.at[turn, k], recv_sem.at[turn, k], 0, side))
        for k, (dx, dy) in enumerate(corners):
            copies.append(remote(csend.at[turn, k], crecv.at[turn, k],
                                 send_sem.at[turn, 4 + k], recv_sem.at[turn, 4 + k], dx, dy))
        for k, side in enumerate(sides):
            mine, theirs = (cx, 0) if side == 1 else (1, cx + 1)
            copies.append(remote(vec.at[:, pl.ds(mine, 1), pl.ds(0, cy), :],
                                 vec.at[:, pl.ds(theirs, 1), pl.ds(0, cy), :],
                                 send_sem.at[turn, 2 + k], recv_sem.at[turn, 2 + k], side, 0))
        return copies

    row_of = {1: rows - 1, -1: cy}
    plane_of = {1: 0, -1: cx + 1}

    def unpack(turn, vec):
        def body(i, _):
            for k, side in enumerate(sides):
                for c in range(3):
                    vec[c, i + 1, pl.ds(row_of[side], 1), :] = yrecv[turn, k, c, pl.ds(i, 1), :]
            return 0

        lax.fori_loop(0, cx, body, 0)
        for k, (dx, dy) in enumerate(corners):
            for c in range(3):
                vec[c, plane_of[dx], pl.ds(row_of[dy], 1), :] = crecv[turn, k, pl.ds(c, 1), :]

    def pack_first(i, _):
        for c in range(3):
            ysend[0, 0, c, pl.ds(i, 1), :] = bvec[c, i + 1, pl.ds(cy - 1, 1), :]
            ysend[0, 1, c, pl.ds(i, 1), :] = bvec[c, i + 1, pl.ds(0, 1), :]
        for e in range(2):
            ysend[0, 0, 3 + e, pl.ds(i, 1), :] = lab[i + 2, pl.ds(cy - 2 + e, 1), :].astype(F32)
        ysend[0, 1, 3, pl.ds(i, 1), :] = lab[i + 2, pl.ds(0, 1), :].astype(F32)
        stiff[i + 2, pl.ds(0, cy), :] = lab[i + 2, pl.ds(0, cy), :].astype(F32)
        return 0

    lax.fori_loop(0, cx, pack_first, 0)

    def label_spots(dx, dy):
        planes = ((cx, 0), (cx + 1, 1)) if dx == 1 else ((2, cx + 2),)
        lines = ((cy - 2, rows - 2), (cy - 1, rows - 1)) if dy == 1 else ((0, cy),)
        return [(p, q) for p in planes for q in lines]

    for k, (dx, dy) in enumerate(corners):
        plane, line = (cx if dx == 1 else 1), (cy - 1 if dy == 1 else 0)
        for c in range(3):
            csend[0, k, pl.ds(c, 1), :] = bvec[c, plane, pl.ds(line, 1), :]
        for e, (p, q) in enumerate(label_spots(dx, dy)):
            csend[0, k, pl.ds(3 + e, 1), :] = lab[p[0], pl.ds(q[0], 1), :].astype(F32)

    pl.semaphore_wait(barrier, n - 1)
    arriving = exchange(0, bvec, (5, 4))
    arriving.append(remote(stiff.at[pl.ds(cx, 2), pl.ds(0, cy), :],
                           stiff.at[pl.ds(0, 2), pl.ds(0, cy), :],
                           lsend_sem.at[0], lrecv_sem.at[0], 1, 0))
    arriving.append(remote(stiff.at[pl.ds(2, 1), pl.ds(0, cy), :],
                           stiff.at[pl.ds(cx + 2, 1), pl.ds(0, cy), :],
                           lsend_sem.at[1], lrecv_sem.at[1], -1, 0))
    for copy in arriving:
        copy.wait_recv()
    unpack(0, bvec)

    def unpack_labels(i, _):
        for e in range(2):
            stiff[i + 2, pl.ds(rows - 2 + e, 1), :] = yrecv[0, 0, 3 + e, pl.ds(i, 1), :]
        stiff[i + 2, pl.ds(cy, 1), :] = yrecv[0, 1, 3, pl.ds(i, 1), :]
        return 0

    lax.fori_loop(0, cx, unpack_labels, 0)
    for k, (dx, dy) in enumerate(corners):
        for e, (p, q) in enumerate(label_spots(dx, dy)):
            stiff[p[1], pl.ds(q[1], 1), :] = crecv[0, k, pl.ds(3 + e, 1), :]

    base, rise = diagonal_weights()

    def prepare(i, _):
        count = stiff[i] + stiff[i + 1]
        count = count + pltpu.roll(count, 1, 0)
        count = count + pltpu.roll(count, 1, 1)
        inverse = 1.0 / (base + rise * count)
        rinv[i] = inverse
        for c in range(3):
            zvec[0, c, i] = bvec[c, i] * inverse
        return 0

    lax.fori_loop(0, cx + 2, prepare, 0)

    for turn in range(ITERS):
        def combine(i, _):
            for c in range(3):
                u = zvec[turn, c, i]
                up = pltpu.roll(u, nz - 1, 1)
                s, d = u + up, up - u
                s_up, d_up = pltpu.roll(s, rows - 1, 0), pltpu.roll(d, rows - 1, 0)
                comb[i, 4 * c] = s + s_up
                comb[i, 4 * c + 1] = s_up - s
                comb[i, 4 * c + 2] = d + d_up
                comb[i, 4 * c + 3] = d_up - d
            return 0

        lax.fori_loop(0, cx + 2, combine, 0)

        for ty in range(rows // 8):
            for tz in range(nz // 128):
                tile = (pl.ds(8 * ty, 8), pl.ds(128 * tz, 128))

                def take(p):
                    return [comb[(p, m) + tile] for m in range(12)]

                first = take(0)
                second = take(1)
                _, high = voxel_forces(first, second, stiff[(1,) + tile])

                def sweep(p, carry):
                    lower, before = carry[:12], carry[12:]
                    upper = take(p + 1)
                    low, high = voxel_forces(lower, upper, stiff[(p + 1,) + tile])
                    for m in range(12):
                        forc[(p - 1, m) + tile] = before[m] + low[m]
                    return tuple(upper) + tuple(high)

                lax.fori_loop(1, cx + 1, sweep, tuple(second) + tuple(high))

        def finish(i, _):
            for c in range(3):
                g = [forc[i, 4 * c + m] for m in range(4)]
                s = (g[0] - g[1]) + pltpu.roll(g[0] + g[1], 1, 0)
                d = (g[2] - g[3]) + pltpu.roll(g[2] + g[3], 1, 0)
                s, d = s[:cy], d[:cy]
                z = zvec[turn, c, i + 1, pl.ds(0, cy), :]
                image = (s - d) + pltpu.roll(s + d, 1, 1) + KAPPA * z
                vvec[turn, c, i] = image
                if turn + 1 < ITERS:
                    new = rinv[i + 1, pl.ds(0, cy), :] * image - SHIFTS[turn] * z
                    if turn > 0:
                        new = new - MIXES[turn] * zvec[turn - 1, c, i + 1, pl.ds(0, cy), :]
                    zvec[turn + 1, c, i + 1, pl.ds(0, cy), :] = new
                    ysend[turn + 1, 0, c, pl.ds(i, 1), :] = new[cy - 1 :]
                    ysend[turn + 1, 1, c, pl.ds(i, 1), :] = new[:1]
            return 0

        lax.fori_loop(0, cx, finish, 0)
        if turn + 1 < ITERS:
            vec = zvec.at[turn + 1]
            for k, (dx, dy) in enumerate(corners):
                plane, line = (cx if dx == 1 else 1), (cy - 1 if dy == 1 else 0)
                for c in range(3):
                    csend[turn + 1, k, pl.ds(c, 1), :] = vec[c, plane, pl.ds(line, 1), :]
            arriving = exchange(turn + 1, vec, (3, 3))
            for copy in arriving:
                copy.wait_recv()
            unpack(turn + 1, vec)

    pairs = [(i, None) for i in range(ITERS)]
    pairs += [(i, j) for j in range(ITERS) for i in range(j + 1)]

    def products(i, carry):
        carry = list(carry)
        for c in range(3):
            zs = [zvec[j, c, i + 1, pl.ds(0, cy), :] for j in range(ITERS)]
            vs = [vvec[j, c, i] for j in range(ITERS)]
            right = bvec[c, i + 1, pl.ds(0, cy), :]
            for k, (a, b) in enumerate(pairs):
                term = zs[a] * (right if b is None else vs[b])
                part = term[:8, :128]
                for ty in range(cy // 8):
                    for tz in range(nz // 128):
                        if ty or tz:
                            part = part + term[8 * ty : 8 * ty + 8, 128 * tz : 128 * tz + 128]
                carry[k] = carry[k] + part
        return tuple(carry)

    sums = lax.fori_loop(0, cx, products,
                         tuple(jnp.zeros((8, 128), F32) for _ in pairs))
    lane = lax.broadcasted_iota(jnp.int32, (1, 128), 1)
    row = jnp.zeros((1, 128), F32)
    for k, part in enumerate(sums):
        line = jnp.sum(part, axis=0, keepdims=True)
        row = jnp.where(lane == k, jnp.sum(line, axis=1, keepdims=True), row)
    psend[...] = row
    precv[me] = row

    def share(k):
        other = lax.rem(me + k, n)
        return pltpu.make_async_remote_copy(
            src_ref=psend, dst_ref=precv.at[me], send_sem=rsend_sem.at[k],
            recv_sem=rrecv_sem.at[k], device_id=(other // ny, lax.rem(other, ny)),
            device_id_type=MESH)

    def start_share(k, _):
        share(k).start()
        return 0

    def end_share(k, _):
        share(k).wait()
        return 0

    lax.fori_loop(1, n, start_share, 0)
    for copy in pending:
        copy.wait_send()
    lax.fori_loop(1, n, end_share, 0)
    total = jnp.sum(precv[...], axis=0)

    picked = {}
    for k, pair in enumerate(pairs):
        picked[pair] = jnp.sum(jnp.where(lane == k, total, 0.0), axis=1, keepdims=True)

    low, inv, scaled, forward = {}, [], {}, []
    for j in range(ITERS):
        for i in range(j):
            w = picked[(i, j)]
            for m in range(i):
                w = w - low[(i, m)] * scaled[(j, m)]
            scaled[(j, i)] = w
            low[(j, i)] = w * inv[i]
        pivot = picked[(j, j)]
        rhs = picked[(j, None)]
        for m in range(j):
            pivot = pivot - low[(j, m)] * scaled[(j, m)]
            rhs = rhs - low[(j, m)] * forward[m]
        sound = pivot > PIVOT_FLOOR * picked[(j, j)]
        inv.append(jnp.where(sound, 1.0 / jnp.where(sound, pivot, 1.0), 0.0))
        forward.append(rhs)
    coef = [None] * ITERS
    for j in reversed(range(ITERS)):
        y = forward[j] * inv[j]
        for i in range(j + 1, ITERS):
            y = y - low[(i, j)] * coef[i]
        coef[j] = y
    wide = [jnp.broadcast_to(y, (cy, nz)) for y in coef]

    def write(i, _):
        for c in range(3):
            x = wide[0] * zvec[0, c, i + 1, pl.ds(0, cy), :]
            r = bvec[c, i + 1, pl.ds(0, cy), :] - wide[0] * vvec[0, c, i]
            for j in range(1, ITERS):
                x = x + wide[j] * zvec[j, c, i + 1, pl.ds(0, cy), :]
                r = r - wide[j] * vvec[j, c, i]
            sol_ref[c, i] = x
            res_ref[c, i] = r
        return 0

    lax.fori_loop(0, cx, write, 0)


def solution(mesh):
    nx, ny = mesh.shape["gx"], mesh.shape["gy"]

    def local(right_side, labels):
        _, cx, cy, nz = right_side.shape
        rows, n = cy + 8, nx * ny
        dma = pltpu.SemaphoreType.DMA
        shape = jax.ShapeDtypeStruct(right_side.shape, F32)
        return tuple(pl.pallas_call(
            functools.partial(cg_kernel, nx, ny, cx, cy, nz),
            out_shape=(shape, shape),
            in_specs=[pl.BlockSpec(memory_space=pl.ANY)] * 2,
            out_specs=(pl.BlockSpec(memory_space=pltpu.VMEM),) * 2,
            scratch_shapes=[
                pltpu.VMEM((3, cx + 2, rows, nz), F32),
                pltpu.VMEM((ITERS, 3, cx + 2, rows, nz), F32),
                pltpu.VMEM((ITERS, 3, cx, cy, nz), F32),
                pltpu.VMEM((cx + 3, rows, nz), jnp.int32),
                pltpu.VMEM((cx + 3, rows, nz), F32),
                pltpu.VMEM((cx + 2, rows, nz), F32),
                pltpu.VMEM((cx + 2, 12, rows, nz), F32),
                pltpu.VMEM((cx, 12, rows, nz), F32),
                pltpu.VMEM((ITERS, 2, 5, cx, nz), F32),
                pltpu.VMEM((ITERS, 2, 5, cx, nz), F32),
                pltpu.VMEM((ITERS, 4, 8, nz), F32),
                pltpu.VMEM((ITERS, 4, 8, nz), F32),
                pltpu.VMEM((1, 128), F32),
                pltpu.VMEM((n, 1, 128), F32),
                dma((2,)), dma((ITERS, 8)), dma((ITERS, 8)), dma((2,)), dma((2,)),
                dma((n,)), dma((n,)),
            ],
            compiler_params=pltpu.CompilerParams(
                collective_id=0, has_side_effects=True, vmem_limit_bytes=48 * 1024 * 1024),
            name="cg",
        )(right_side, labels))

    in_specs = (P(None, "gx", "gy", None), P("gx", "gy", None))
    out_specs = (P(None, "gx", "gy", None), P(None, "gx", "gy", None))
    return jax.shard_map(local, mesh=mesh, in_specs=in_specs, out_specs=out_specs, check_vma=False)
```

```python
import functools
import math

import jax
import jax.numpy as jnp
import numpy as np
from jax import lax
from jax.experimental import pallas as pl
from jax.experimental.pallas import tpu as pltpu
from jax.sharding import PartitionSpec as P

ITERS = 4

LAMBDA_SOFT = 0.5769231
LAMBDA_RISE = 1.6452991
SHEAR_SOFT = 0.3846154
SHEAR_RISE = 2.9487179
KAPPA = 0.05
PIVOT_FLOOR = 1e-6
SHIFTS = (1.0, 1.4, 1.4)
MIXES = (0.0, 0.3, 0.45)

MESH = pl.DeviceIdType.MESH
F32 = jnp.float32


def corner_bits(corner):
    return (corner >> 2 & 1, corner >> 1 & 1, corner & 1)


def element_tables():
    gauss_offset = 0.5 / math.sqrt(3.0)
    gauss_points = [0.5 - gauss_offset, 0.5 + gauss_offset]
    lame_table = np.zeros((24, 24))
    shear_table = np.zeros((24, 24))
    normal_block = np.zeros((6, 6))
    normal_block[:3, :3] = 1.0
    shear_block = np.diag([2.0, 2.0, 2.0, 1.0, 1.0, 1.0])
    for point_x in gauss_points:
        for point_y in gauss_points:
            for point_z in gauss_points:
                strain = np.zeros((6, 24))
                for corner in range(8):
                    cx_bit, cy_bit, cz_bit = corner_bits(corner)
                    shape_x = point_x if cx_bit else 1.0 - point_x
                    shape_y = point_y if cy_bit else 1.0 - point_y
                    shape_z = point_z if cz_bit else 1.0 - point_z
                    slope_x = 1.0 if cx_bit else -1.0
                    slope_y = 1.0 if cy_bit else -1.0
                    slope_z = 1.0 if cz_bit else -1.0
                    grad_x = slope_x * shape_y * shape_z
                    grad_y = shape_x * slope_y * shape_z
                    grad_z = shape_x * shape_y * slope_z
                    column = 3 * corner
                    strain[0, column] = grad_x
                    strain[1, column + 1] = grad_y
                    strain[2, column + 2] = grad_z
                    strain[3, column + 1] = grad_z
                    strain[3, column + 2] = grad_y
                    strain[4, column] = grad_z
                    strain[4, column + 2] = grad_x
                    strain[5, column] = grad_y
                    strain[5, column + 1] = grad_x
                lame_table += 0.125 * strain.T @ normal_block @ strain
                shear_table += 0.125 * strain.T @ shear_block @ strain
    return lame_table, shear_table


def diagonal_weights():
    lame_table, shear_table = element_tables()
    lame, shear = np.diag(lame_table), np.diag(shear_table)
    assert np.allclose(lame, lame[0]) and np.allclose(shear, shear[0])
    soft = LAMBDA_SOFT * lame[0] + SHEAR_SOFT * shear[0]
    rise = LAMBDA_RISE * lame[0] + SHEAR_RISE * shear[0]
    return float(8.0 * soft + KAPPA), float(rise)


def voxel_forces(lower, upper, stiff):
    l0 = LAMBDA_SOFT / 16.0 + LAMBDA_RISE / 16.0 * stiff
    m0 = SHEAR_SOFT / 16.0 + SHEAR_RISE / 16.0 * stiff
    l1, m1 = l0 * (1.0 / 3.0), m0 * (1.0 / 3.0)
    q = (l1 + 4.0 * m1) * (1.0 / 3.0)
    m0_2 = m0 + m0
    m1_3 = m0
    fx, fy, fz, fxy, fxz, fyz, fxyz = ([None] * 3 for _ in range(7))
    ex, ey, ez, exy, exz, eyz = ([None] * 3 for _ in range(6))
    for c in range(3):
        a, b = lower[4 * c : 4 * c + 4], upper[4 * c : 4 * c + 4]
        ex[c] = b[0] - a[0]
        ey[c], exy[c] = a[1] + b[1], b[1] - a[1]
        ez[c], exz[c] = a[2] + b[2], b[2] - a[2]
        eyz[c] = a[3] + b[3]
        fxyz[c] = q * (b[3] - a[3])
    trace = l0 * (ex[0] + ey[1] + ez[2])
    fx[0] = trace + m0_2 * ex[0]
    fy[1] = trace + m0_2 * ey[1]
    fz[2] = trace + m0_2 * ez[2]
    fy[0] = fx[1] = m0 * (ey[0] + ex[1])
    fz[0] = fx[2] = m0 * (ez[0] + ex[2])
    fz[1] = fy[2] = m0 * (ez[1] + ey[2])
    part = l1 * (exy[0] + eyz[2])
    fxy[0], fyz[2] = part + m1_3 * exy[0], part + m1_3 * eyz[2]
    part = l1 * (exy[1] + exz[2])
    fxy[1], fxz[2] = part + m1_3 * exy[1], part + m1_3 * exz[2]
    part = l1 * (exz[0] + eyz[1])
    fxz[0], fyz[1] = part + m1_3 * exz[0], part + m1_3 * eyz[1]
    total = eyz[0] + exz[1] + exy[2]
    fyz[0] = m1 * (total + eyz[0])
    fxz[1] = m1 * (total + exz[1])
    fxy[2] = m1 * (total + exy[2])
    low, high = [], []
    for c in range(3):
        low += [-fx[c], fy[c] - fxy[c], fz[c] - fxz[c], fyz[c] - fxyz[c]]
        high += [fx[c], fy[c] + fxy[c], fz[c] + fxz[c], fyz[c] + fxyz[c]]
    return low, high


def loop(first, last, body, init, by):
    by = math.gcd(last - first, by)

    def trip(k, carry):
        for step in range(by):
            carry = body(first + k * by + step, carry)
        return carry

    return lax.fori_loop(0, (last - first) // by, trip, init)


def cg_kernel(nx, ny, cx, cy, nz, rhs_hbm, lab_hbm, sol_ref, res_ref,
              bvec, zvec, vvec, lab, stiff, rinv, comb, forc, ysend, yrecv, csend, crecv,
              psend, precv, in_sem, send_sem, recv_sem, lsend_sem, lrecv_sem,
              rsend_sem, rrecv_sem):
    rows = cy + 8
    n = nx * ny
    gx, gy = lax.axis_index("gx"), lax.axis_index("gy")
    me = gx * ny + gy
    xs = {-1: lax.rem(gx + nx - 1, nx), 0: gx, 1: lax.rem(gx + 1, nx)}
    ys = {-1: lax.rem(gy + ny - 1, ny), 0: gy, 1: lax.rem(gy + 1, ny)}

    load_b = pltpu.make_async_copy(
        rhs_hbm, bvec.at[:, pl.ds(1, cx), pl.ds(0, cy), :], in_sem.at[0])
    load_l = pltpu.make_async_copy(
        lab_hbm, lab.at[pl.ds(2, cx), pl.ds(0, cy), :], in_sem.at[1])
    load_b.start()
    load_l.start()

    barrier = pltpu.get_barrier_semaphore()

    def greet(k, _):
        other = lax.rem(me + k, n)
        pl.semaphore_signal(barrier, inc=1, device_id=(other // ny, lax.rem(other, ny)),
                            device_id_type=MESH)
        return 0

    lax.fori_loop(1, n, greet, 0)
    load_b.wait()
    load_l.wait()

    sides = (1, -1)
    corners = ((1, 1), (1, -1), (-1, 1), (-1, -1))
    pending = []

    def remote(src, dst, s_sem, r_sem, dx, dy):
        copy = pltpu.make_async_remote_copy(
            src_ref=src, dst_ref=dst, send_sem=s_sem, recv_sem=r_sem,
            device_id=(xs[dx], ys[dy]), device_id_type=MESH)
        copy.start()
        pending.append(copy)
        return copy

    def exchange(turn, vec, depth):
        copies = []
        for k, side in enumerate(sides):
            parts = depth[k]
            copies.append(remote(ysend.at[turn, k, pl.ds(0, parts)],
                                 yrecv.at[turn, k, pl.ds(0, parts)],
                                 send_sem.at[turn, k], recv_sem.at[turn, k], 0, side))
        for k, (dx, dy) in enumerate(corners):
            copies.append(remote(csend.at[turn, k], crecv.at[turn, k],
                                 send_sem.at[turn, 4 + k], recv_sem.at[turn, 4 + k], dx, dy))
        for k, side in enumerate(sides):
            mine, theirs = (cx, 0) if side == 1 else (1, cx + 1)
            copies.append(remote(vec.at[:, pl.ds(mine, 1), pl.ds(0, cy), :],
                                 vec.at[:, pl.ds(theirs, 1), pl.ds(0, cy), :],
                                 send_sem.at[turn, 2 + k], recv_sem.at[turn, 2 + k], side, 0))
        return copies

    row_of = {1: rows - 1, -1: cy}
    plane_of = {1: 0, -1: cx + 1}

    def unpack(turn, vec):
        def body(i, _):
            for k, side in enumerate(sides):
                for c in range(3):
                    vec[c, i + 1, pl.ds(row_of[side], 1), :] = yrecv[turn, k, c, pl.ds(i, 1), :]
            return 0

        loop(0, cx, body, 0, 8)
        for k, (dx, dy) in enumerate(corners):
            for c in range(3):
                vec[c, plane_of[dx], pl.ds(row_of[dy], 1), :] = crecv[turn, k, pl.ds(c, 1), :]

    def pack_first(i, _):
        for c in range(3):
            ysend[0, 0, c, pl.ds(i, 1), :] = bvec[c, i + 1, pl.ds(cy - 1, 1), :]
            ysend[0, 1, c, pl.ds(i, 1), :] = bvec[c, i + 1, pl.ds(0, 1), :]
        for e in range(2):
            ysend[0, 0, 3 + e, pl.ds(i, 1), :] = lab[i + 2, pl.ds(cy - 2 + e, 1), :].astype(F32)
        ysend[0, 1, 3, pl.ds(i, 1), :] = lab[i + 2, pl.ds(0, 1), :].astype(F32)
        stiff[i + 2, pl.ds(0, cy), :] = lab[i + 2, pl.ds(0, cy), :].astype(F32)
        return 0

    loop(0, cx, pack_first, 0, 4)

    def label_spots(dx, dy):
        planes = ((cx, 0), (cx + 1, 1)) if dx == 1 else ((2, cx + 2),)
        lines = ((cy - 2, rows - 2), (cy - 1, rows - 1)) if dy == 1 else ((0, cy),)
        return [(p, q) for p in planes for q in lines]

    for k, (dx, dy) in enumerate(corners):
        plane, line = (cx if dx == 1 else 1), (cy - 1 if dy == 1 else 0)
        for c in range(3):
            csend[0, k, pl.ds(c, 1), :] = bvec[c, plane, pl.ds(line, 1), :]
        for e, (p, q) in enumerate(label_spots(dx, dy)):
            csend[0, k, pl.ds(3 + e, 1), :] = lab[p[0], pl.ds(q[0], 1), :].astype(F32)

    pl.semaphore_wait(barrier, n - 1)
    arriving = exchange(0, bvec, (5, 4))
    arriving.append(remote(stiff.at[pl.ds(cx, 2), pl.ds(0, cy), :],
                           stiff.at[pl.ds(0, 2), pl.ds(0, cy), :],
                           lsend_sem.at[0], lrecv_sem.at[0], 1, 0))
    arriving.append(remote(stiff.at[pl.ds(2, 1), pl.ds(0, cy), :],
                           stiff.at[pl.ds(cx + 2, 1), pl.ds(0, cy), :],
                           lsend_sem.at[1], lrecv_sem.at[1], -1, 0))
    for copy in arriving:
        copy.wait_recv()
    unpack(0, bvec)

    def unpack_labels(i, _):
        for e in range(2):
            stiff[i + 2, pl.ds(rows - 2 + e, 1), :] = yrecv[0, 0, 3 + e, pl.ds(i, 1), :]
        stiff[i + 2, pl.ds(cy, 1), :] = yrecv[0, 1, 3, pl.ds(i, 1), :]
        return 0

    loop(0, cx, unpack_labels, 0, 8)
    for k, (dx, dy) in enumerate(corners):
        for e, (p, q) in enumerate(label_spots(dx, dy)):
            stiff[p[1], pl.ds(q[1], 1), :] = crecv[0, k, pl.ds(3 + e, 1), :]

    base, rise = diagonal_weights()

    def prepare(i, _):
        count = stiff[i] + stiff[i + 1]
        count = count + pltpu.roll(count, 1, 0)
        count = count + pltpu.roll(count, 1, 1)
        inverse = 1.0 / (base + rise * count)
        rinv[i] = inverse
        for c in range(3):
            zvec[0, c, i] = bvec[c, i] * inverse
        return 0

    loop(0, cx + 2, prepare, 0, 3)

    pairs, sums = [], []

    def add_products(turn):
        def products(i, carry):
            carry = list(carry)
            for c in range(3):
                right = bvec[c, i + 1, pl.ds(0, cy), :]
                image = vvec[turn, c, i]
                for k in range(turn + 2):
                    if k <= turn:
                        term = zvec[k, c, i + 1, pl.ds(0, cy), :] * image
                    else:
                        term = zvec[turn, c, i + 1, pl.ds(0, cy), :] * right
                    for ty in range(cy // 8):
                        for tz in range(nz // 128):
                            carry[k] += term[8 * ty : 8 * ty + 8, 128 * tz : 128 * tz + 128]
            return tuple(carry)

        zero = jnp.zeros((8, 128), F32)
        sums.extend(loop(0, cx, products, (zero,) * (turn + 2), 2))
        pairs.extend([(k, turn) for k in range(turn + 1)] + [(turn, None)])

    for turn in range(ITERS):
        def combine(i, _):
            for c in range(3):
                u = zvec[turn, c, i]
                up = pltpu.roll(u, nz - 1, 1)
                s, d = u + up, up - u
                s_up, d_up = pltpu.roll(s, rows - 1, 0), pltpu.roll(d, rows - 1, 0)
                comb[i, 4 * c] = s + s_up
                comb[i, 4 * c + 1] = s_up - s
                comb[i, 4 * c + 2] = d + d_up
                comb[i, 4 * c + 3] = d_up - d
            return 0

        loop(0, cx + 2, combine, 0, 3)

        for ty in range(rows // 8):
            for tz in range(nz // 128):
                tile = (pl.ds(8 * ty, 8), pl.ds(128 * tz, 128))

                def take(p):
                    return [comb[(p, m) + tile] for m in range(12)]

                first = take(0)
                second = take(1)
                _, high = voxel_forces(first, second, stiff[(1,) + tile])

                def sweep(p, carry):
                    lower, before = carry[:12], carry[12:]
                    upper = take(p + 1)
                    low, high = voxel_forces(lower, upper, stiff[(p + 1,) + tile])
                    for m in range(12):
                        forc[(p - 1, m) + tile] = before[m] + low[m]
                    return tuple(upper) + tuple(high)

                loop(1, cx + 1, sweep, tuple(second) + tuple(high), 4)

        def finish(i, _):
            for c in range(3):
                g = [forc[i, 4 * c + m] for m in range(4)]
                s = (g[0] - g[1]) + pltpu.roll(g[0] + g[1], 1, 0)
                d = (g[2] - g[3]) + pltpu.roll(g[2] + g[3], 1, 0)
                s, d = s[:cy], d[:cy]
                z = zvec[turn, c, i + 1, pl.ds(0, cy), :]
                image = (s - d) + pltpu.roll(s + d, 1, 1) + KAPPA * z
                vvec[turn, c, i] = image
                if turn + 1 < ITERS:
                    new = rinv[i + 1, pl.ds(0, cy), :] * image - SHIFTS[turn] * z
                    if turn > 0:
                        new = new - MIXES[turn] * zvec[turn - 1, c, i + 1, pl.ds(0, cy), :]
                    zvec[turn + 1, c, i + 1, pl.ds(0, cy), :] = new
                    ysend[turn + 1, 0, c, pl.ds(i, 1), :] = new[cy - 1 :]
                    ysend[turn + 1, 1, c, pl.ds(i, 1), :] = new[:1]
            return 0

        loop(0, cx, finish, 0, 4)
        if turn + 1 < ITERS:
            vec = zvec.at[turn + 1]
            for k, (dx, dy) in enumerate(corners):
                plane, line = (cx if dx == 1 else 1), (cy - 1 if dy == 1 else 0)
                for c in range(3):
                    csend[turn + 1, k, pl.ds(c, 1), :] = vec[c, plane, pl.ds(line, 1), :]
            arriving = exchange(turn + 1, vec, (3, 3))
            add_products(turn)
            for copy in arriving:
                copy.wait_recv()
            unpack(turn + 1, vec)

    add_products(ITERS - 1)
    lane = lax.broadcasted_iota(jnp.int32, (1, 128), 1)
    row = jnp.zeros((1, 128), F32)
    for k, part in enumerate(sums):
        line = jnp.sum(part, axis=0, keepdims=True)
        row = jnp.where(lane == k, jnp.sum(line, axis=1, keepdims=True), row)
    psend[...] = row
    precv[me] = row

    def share(k):
        other = lax.rem(me + k, n)
        return pltpu.make_async_remote_copy(
            src_ref=psend, dst_ref=precv.at[me], send_sem=rsend_sem.at[k],
            recv_sem=rrecv_sem.at[k], device_id=(other // ny, lax.rem(other, ny)),
            device_id_type=MESH)

    def start_share(k, _):
        share(k).start()
        return 0

    def end_share(k, _):
        share(k).wait()
        return 0

    lax.fori_loop(1, n, start_share, 0)
    for copy in pending:
        copy.wait_send()
    lax.fori_loop(1, n, end_share, 0)
    total = jnp.sum(precv[...], axis=0)

    picked = {}
    for k, pair in enumerate(pairs):
        picked[pair] = jnp.sum(jnp.where(lane == k, total, 0.0), axis=1, keepdims=True)

    low, inv, scaled, forward = {}, [], {}, []
    for j in range(ITERS):
        for i in range(j):
            w = picked[(i, j)]
            for m in range(i):
                w = w - low[(i, m)] * scaled[(j, m)]
            scaled[(j, i)] = w
            low[(j, i)] = w * inv[i]
        pivot = picked[(j, j)]
        rhs = picked[(j, None)]
        for m in range(j):
            pivot = pivot - low[(j, m)] * scaled[(j, m)]
            rhs = rhs - low[(j, m)] * forward[m]
        sound = pivot > PIVOT_FLOOR * picked[(j, j)]
        inv.append(jnp.where(sound, 1.0 / jnp.where(sound, pivot, 1.0), 0.0))
        forward.append(rhs)
    coef = [None] * ITERS
    for j in reversed(range(ITERS)):
        y = forward[j] * inv[j]
        for i in range(j + 1, ITERS):
            y = y - low[(i, j)] * coef[i]
        coef[j] = y
    wide = [jnp.broadcast_to(y, (cy, nz)) for y in coef]

    def write(i, _):
        for c in range(3):
            x = wide[0] * zvec[0, c, i + 1, pl.ds(0, cy), :]
            r = bvec[c, i + 1, pl.ds(0, cy), :] - wide[0] * vvec[0, c, i]
            for j in range(1, ITERS):
                x = x + wide[j] * zvec[j, c, i + 1, pl.ds(0, cy), :]
                r = r - wide[j] * vvec[j, c, i]
            sol_ref[c, i] = x
            res_ref[c, i] = r
        return 0

    loop(0, cx, write, 0, 4)


def solution(mesh):
    nx, ny = mesh.shape["gx"], mesh.shape["gy"]

    def local(right_side, labels):
        _, cx, cy, nz = right_side.shape
        rows, n = cy + 8, nx * ny
        dma = pltpu.SemaphoreType.DMA
        shape = jax.ShapeDtypeStruct(right_side.shape, F32)
        return tuple(pl.pallas_call(
            functools.partial(cg_kernel, nx, ny, cx, cy, nz),
            out_shape=(shape, shape),
            in_specs=[pl.BlockSpec(memory_space=pl.ANY)] * 2,
            out_specs=(pl.BlockSpec(memory_space=pltpu.VMEM),) * 2,
            scratch_shapes=[
                pltpu.VMEM((3, cx + 2, rows, nz), F32),
                pltpu.VMEM((ITERS, 3, cx + 2, rows, nz), F32),
                pltpu.VMEM((ITERS, 3, cx, cy, nz), F32),
                pltpu.VMEM((cx + 3, rows, nz), jnp.int32),
                pltpu.VMEM((cx + 3, rows, nz), F32),
                pltpu.VMEM((cx + 2, rows, nz), F32),
                pltpu.VMEM((cx + 2, 12, rows, nz), F32),
                pltpu.VMEM((cx, 12, rows, nz), F32),
                pltpu.VMEM((ITERS, 2, 5, cx, nz), F32),
                pltpu.VMEM((ITERS, 2, 5, cx, nz), F32),
                pltpu.VMEM((ITERS, 4, 8, nz), F32),
                pltpu.VMEM((ITERS, 4, 8, nz), F32),
                pltpu.VMEM((1, 128), F32),
                pltpu.VMEM((n, 1, 128), F32),
                dma((2,)), dma((ITERS, 8)), dma((ITERS, 8)), dma((2,)), dma((2,)),
                dma((n,)), dma((n,)),
            ],
            compiler_params=pltpu.CompilerParams(
                collective_id=0, has_side_effects=True, vmem_limit_bytes=48 * 1024 * 1024),
            name="cg",
        )(right_side, labels))

    in_specs = (P(None, "gx", "gy", None), P("gx", "gy", None))
    out_specs = (P(None, "gx", "gy", None), P(None, "gx", "gy", None))
    return jax.shard_map(local, mesh=mesh, in_specs=in_specs, out_specs=out_specs, check_vma=False)
```
